32 devices in a mesh: samp: 1, vert: 32 (over z, y, x, core).
Axes of the slice: x: 2, y: 2, z: 4, core: 2. Of those that a mesh axis runs over, the one named last changes fastest.
Arguments:
- inputs: bfloat16 [2, 131072, 128], P('samp', 'vert'), may hold values from -6 to 6
- cotangent: bfloat16 [2, 131072, 128], P('samp', 'vert'), may hold values from -6 to 6
- basis: bfloat16 [131072, 1024], P('vert'), may hold values from -0.03125 to 0.03125
- mode_weights: bfloat16 [1024, 128, 128], P('vert'), may hold values from -0.5 to 0.5
- w_up: bfloat16 [128, 512], replicated, may hold values from -0.5 to 0.5
- b_up: float32 [512], replicated, may hold values from -4 to 4
- w_down: bfloat16 [512, 128], replicated, may hold values from -0.25 to 0.25
Outputs:
- grad_input: bfloat16 [2, 131072, 128], P('samp', 'vert')
- grad_modes: float32 [1024, 128, 128], P('vert')
- grad_w_up: float32 [128, 512], replicated
- grad_b_up: float32 [512], replicated
- grad_w_down: float32 [512, 128], replicated
The draws below stay inside these ranges and needn't reach their ends.
All inputs are finite; a program needn't handle non-finite values.
Results may differ from the reference program's by a relative error of at most 0.0055.
Values may be sent and summed in bfloat16 or wider, within the bound.
A program may use at most 128 MiB of HBM per device.

```python
import jax
import jax.numpy as jnp
from jax import lax

C = 128
H = 512
K = 1024
VERTICES = 131072
SAMPLES = 2


def shard_levels(stream_key, extent, pieces, smallest, top_value):
    level, own = 1.0, jax.random.fold_in(stream_key, 6)
    for axis_at, blocks in pieces:
        steps = jnp.exp(jax.random.uniform(jax.random.fold_in(own, axis_at), (blocks,), jnp.float32, smallest / len(pieces), top_value / len(pieces)))
        level = level * jnp.repeat(steps, extent[axis_at] // blocks).reshape([-1 if axis == axis_at else 1 for axis in range(len(extent))])
    return level


def normal_values(own_key, dims, scale, most, shards=(), held_as=jnp.bfloat16):
    loudness = shard_levels(own_key, dims, shards, -0.22, 0.18) if shards else 1.0
    entries = jax.random.normal(own_key, dims, jnp.float32) * scale * loudness
    return jnp.minimum(jnp.maximum(entries, -most), most).astype(held_as)


def setup_inputs(seed: int = 0) -> dict:
    seeds = jax.random.split(jax.random.key(seed), 8)
    return {
        "inputs": normal_values(seeds[0], (SAMPLES, VERTICES, C), 1.0, 6.0, ((1, 32),)),
        "cotangent": normal_values(seeds[1], (SAMPLES, VERTICES, C), 1.0, 6.0, ((1, 32),)),
        "basis": normal_values(seeds[2], (VERTICES, K), (VERTICES // 4) ** -0.5, 0.03125, ((0, 32),)),
        "mode_weights": normal_values(seeds[3], (K, C, C), C ** -0.5, 0.5, ((0, 32),)),
        "w_up": normal_values(seeds[4], (C, H), C ** -0.5, 0.5),
        "b_up": normal_values(seeds[5], (H,), 1.0, 4.0, (), jnp.float32),
        "w_down": normal_values(seeds[6], (H, C), H ** -0.5, 0.25),
    }


def gelu_value(pre_act):
    inner = 0.7978845608 * (pre_act + 0.044715 * pre_act * pre_act * pre_act)
    return 0.5 * pre_act * (1.0 + jnp.tanh(inner))


def gelu_slope(pre_act):
    inner = 0.7978845608 * (pre_act + 0.044715 * pre_act * pre_act * pre_act)
    tangent = jnp.tanh(inner)
    return 0.5 * (1.0 + tangent) + 0.5 * pre_act * (1.0 - tangent * tangent) * 0.7978845608 * (1.0 + 3.0 * 0.044715 * pre_act * pre_act)


def reference(inputs, cotangent, basis, mode_weights, w_up, b_up, w_down):
    mixing = mode_weights.astype(jnp.float32)
    grad_modes = jnp.zeros((K, C, C), jnp.float32)
    grad_w_up = jnp.zeros((C, H), jnp.float32)
    grad_b_up = jnp.zeros((H,), jnp.float32)
    grad_w_down = jnp.zeros((H, C), jnp.float32)
    results = []
    for sample in range(SAMPLES):
        coeffs = jnp.dot(basis.T, inputs[sample], preferred_element_type=jnp.float32)
        grad_out = jnp.dot(basis.T, cotangent[sample], preferred_element_type=jnp.float32)
        grad_coef = jnp.einsum("kd,kcd->kc", grad_out, mixing, precision=lax.Precision.HIGHEST).astype(jnp.bfloat16)
        grad_modes = grad_modes + jnp.einsum("kc,kd->kcd", coeffs, grad_out, precision=lax.Precision.HIGHEST)
        spectral = jnp.dot(basis, grad_coef, preferred_element_type=jnp.float32)
        pre_act = jnp.dot(inputs[sample], w_up, preferred_element_type=jnp.float32) + b_up
        hidden = gelu_value(pre_act).astype(jnp.bfloat16)
        grad_hidden = jnp.dot(cotangent[sample], w_down.T, preferred_element_type=jnp.float32)
        grad_pre = (grad_hidden * gelu_slope(pre_act)).astype(jnp.bfloat16)
        pointwise = jnp.dot(grad_pre, w_up.T, preferred_element_type=jnp.float32)
        results.append((spectral + pointwise).astype(jnp.bfloat16))
        grad_w_up = grad_w_up + jnp.dot(inputs[sample].T, grad_pre, preferred_element_type=jnp.float32)
        grad_b_up = grad_b_up + jnp.sum(grad_pre.astype(jnp.float32), axis=0)
        grad_w_down = grad_w_down + jnp.dot(hidden.T, cotangent[sample], preferred_element_type=jnp.float32)
    grad_input = jnp.stack(results, axis=0)
    return (grad_input, grad_modes, grad_w_up, grad_b_up, grad_w_down)
```

```python
import functools

import jax
import jax.numpy as jnp
from jax import lax
from jax.experimental import pallas as pl
from jax.experimental.pallas import tpu as pltpu
from jax.sharding import PartitionSpec as P

F32 = jnp.float32
BF16 = jnp.bfloat16
MESH = pl.DeviceIdType.MESH
ROOT = 0.7978845608
CUBE = 0.044715


def reduce_radices(size):
    return (size // 8, 4, 2) if size % 16 == 0 else gather_radices(size)


def gather_radices(size):
    return (size // 2, 2) if size % 4 == 0 else (size,)


def staged(radices, size):
    left, found = size, []
    for radix in reversed(radices):
        left //= radix
        found.append((radix, left))
    return found


def dot(left, right, contract):
    return lax.dot_general(left, right, (contract, ((), ())), preferred_element_type=F32)


class Grid:
    def __init__(self, me, radices):
        self.me, self.radices, self.depth = me, radices, len(radices)
        self.strides = [1] * self.depth
        for at in range(self.depth - 2, -1, -1):
            self.strides[at] = self.strides[at + 1] * radices[at + 1]
        self.digits = [lax.rem(lax.div(me, self.strides[at]), radices[at]) for at in range(self.depth)]
        self.order = tuple(reversed(range(self.depth)))
        self.mine = tuple(self.digits[at] for at in self.order)

    def peer(self, at, shift):
        digit = lax.rem(self.digits[at] + shift, self.radices[at])
        return digit, {"vert": self.me + (digit - self.digits[at]) * self.strides[at]}

    def digits_of(self, owner):
        return tuple((owner // self.strides[at]) % self.radices[at] for at in self.order)

    def slot_of(self, owner):
        found = self.digits_of(owner)
        rest, scale = 0, 1
        for at, digit in zip(self.order[1:], found[1:]):
            rest += digit * scale
            scale *= self.radices[at]
        return found[0], rest


def layer_kernel(
    plan,
    inputs_hbm, cotangent_hbm, basis_hbm, modes_hbm, w_up_hbm, b_up_hbm, w_down_hbm,
    grad_input, grad_modes, grad_up, grad_bias, grad_down,
    xs, cs, xt, basis, modes, w_up, b_up, w_down, acc, pointwise,
    up_acc, down_acc, bias_acc, gathered, natural, left_rows, right_rows, mixed,
    weights_all, in_sems, send_sems, recv_sems, *stages,
):
    size = plan["size"]
    samples, here, chan = xs.shape
    hidden_units = w_up.shape[1]
    total_modes = basis.shape[1]
    owned = total_modes // size
    me = lax.axis_index("vert")
    reduce, gather = Grid(me, plan["reduce"]), Grid(me, plan["gather"])
    pool = list(stages)

    def take(count):
        found = pool[:count]
        del pool[:count]
        return found

    coef_held = [take(reduce.depth) for _ in range(samples)]
    coef_sent = [take(reduce.depth) for _ in range(samples)]
    coef_got = [take(reduce.depth) for _ in range(samples)]
    weight_held, weight_sent, weight_got = take(gather.depth), take(gather.depth), take(gather.depth)
    bias_slots = take(gather.depth)

    load_steps = plan["load_steps"]
    load_rows = here // load_steps

    def row_block(step):
        return pl.ds(pl.multiple_of(step * load_rows, load_rows), load_rows)

    def field_loads(s, step):
        rows = row_block(step)
        return (
            pltpu.make_async_copy(inputs_hbm.at[s, rows], xs.at[s, rows], in_sems.at[2 * s, step]),
            pltpu.make_async_copy(cotangent_hbm.at[s, rows], cs.at[s, rows], in_sems.at[2 * s + 1, step]),
        )

    def basis_load(step):
        rows = row_block(step)
        return pltpu.make_async_copy(basis_hbm.at[rows], basis.at[rows], in_sems.at[2 * samples, step])

    small_copies = [
        pltpu.make_async_copy(source, target, in_sems.at[2 * samples + 1 + at, 0])
        for at, (source, target) in enumerate(
            ((w_up_hbm, w_up), (b_up_hbm, b_up), (w_down_hbm, w_down), (modes_hbm, modes)))
    ]
    for step in range(load_steps):
        for copy in field_loads(0, step):
            copy.start()
        basis_load(step).start()
    for s in range(1, samples):
        for step in range(load_steps):
            for copy in field_loads(s, step):
                copy.start()
    for copy in small_copies:
        copy.start()

    barrier = pltpu.get_barrier_semaphore()
    peers = 0
    for at in range(gather.depth):
        for shift in range(1, gather.radices[at]):
            pl.semaphore_signal(barrier, inc=1, device_id=gather.peer(at, shift)[1], device_id_type=MESH)
            peers += 1

    acc[...] = jnp.zeros_like(acc)
    up_acc[...] = jnp.zeros_like(up_acc)
    down_acc[...] = jnp.zeros_like(down_acc)
    bias_acc[...] = jnp.zeros_like(bias_acc)
    left_rows[...] = jnp.zeros_like(left_rows)
    right_rows[...] = jnp.zeros_like(right_rows)

    sem_at = [0]

    def exchange(grid, at, pairs):
        copies = []
        for shift in range(1, grid.radices[at]):
            digit, target = grid.peer(at, shift)
            for source_of, dest in pairs:
                copies.append(pltpu.make_async_remote_copy(
                    src_ref=source_of(digit),
                    dst_ref=dest,
                    send_sem=send_sems.at[sem_at[0]],
                    recv_sem=recv_sems.at[sem_at[0]],
                    device_id=target,
                    device_id_type=MESH,
                ))
                sem_at[0] += 1
        for copy in copies:
            copy.start()
        return copies

    def finish(copies):
        for copy in copies:
            copy.wait()

    def scatter_start(grid, turn, held, sent, got):
        at = grid.order[turn]
        source = (held if turn == 0 else sent)[turn]
        return exchange(grid, at, [(lambda digit: source.at[digit], got[turn].at[grid.digits[at]])])

    def scatter_sum(grid, turn, copies, held, sent, got):
        finish(copies)
        at = grid.order[turn]
        for block in range(held[turn].shape[1]):
            value = held[turn][grid.digits[at], block]
            for shift in range(1, grid.radices[at]):
                value = value + got[turn][grid.peer(at, shift)[0], block].astype(F32)
            if turn + 1 == grid.depth:
                return value
            radix = grid.radices[grid.order[turn + 1]]
            held[turn + 1][block % radix, block // radix] = value
            sent[turn + 1][block % radix, block // radix] = value.astype(BF16)

    def gather_start(grid, turn, ref):
        held = ref.at[grid.mine[:grid.depth - turn]]
        return exchange(grid, grid.order[grid.depth - 1 - turn], [(lambda digit: held, held)])

    chunk = plan["chunk"]
    chunks = here // chunk
    done_chunks = [0]

    def point(step, carry):
        rows = pl.ds(pl.multiple_of(step * chunk, chunk), chunk)
        for s in range(samples):
            z = dot(xs[s, rows, :], w_up[...], ((1,), (0,))) + b_up[...]
            square = z * z
            t = jnp.tanh(z * (ROOT + (ROOT * CUBE) * square))
            middle = 0.5 * z
            plus = 1.0 + t
            hidden = (middle * plus).astype(BF16)
            slope = plus * (0.5 + middle * (1.0 - t) * (ROOT + (3.0 * ROOT * CUBE) * square))
            grad_hidden = dot(cs[s, rows, :], w_down[...], ((1,), (1,)))
            grad_pre = (grad_hidden * slope).astype(BF16)
            pointwise[s, rows, :] = dot(grad_pre, w_up[...], ((1,), (1,)))
            up_acc[...] += dot(xt[2 * s * chan:(2 * s + 1) * chan, rows], grad_pre, ((1,), (0,)))
            down_acc[...] += dot(xt[(2 * s + 1) * chan:(2 * s + 2) * chan, rows], hidden, ((1,), (0,)))
            bias_acc[...] += jnp.sum(grad_pre.astype(F32).reshape(chunk // 8, 8, hidden_units), axis=0)
        return carry

    def work(count):
        first = done_chunks[0]
        last = min(chunks, first + count)
        done_chunks[0] = last
        if last > first:
            lax.fori_loop(first, last, point, 0)

    coef_copies = [None] * samples

    def coef_start(s, turn):
        coef_copies[s] = scatter_start(reduce, turn, coef_held[s], coef_sent[s], coef_got[s])

    def coef_sum(s, turn):
        return scatter_sum(reduce, turn, coef_copies[s], coef_held[s], coef_sent[s], coef_got[s])

    for s in range(samples):
        def project(step, carry):
            if s == 0:
                basis_load(step).wait()
            for copy in field_loads(s, step):
                copy.wait()
            rows = row_block(step)
            low = 2 * s * chan
            xt[low:low + chan, rows] = xs[s, rows, :].T
            xt[low + chan:low + 2 * chan, rows] = cs[s, rows, :].T
            acc[low:low + 2 * chan] += dot(xt[low:low + 2 * chan, rows], basis[rows, :], ((1,), (0,)))
            return carry

        lax.fori_loop(0, load_steps, project, 0)
        if s == 0:
            pl.semaphore_wait(barrier, peers)
        for block in range(total_modes // 128):
            tile = acc[2 * s * chan:2 * (s + 1) * chan, block * 128:(block + 1) * 128].T
            for part in range(128 // owned):
                owner = block * (128 // owned) + part
                coef_held[s][0][reduce.slot_of(owner)] = tile[part * owned:(part + 1) * owned]
        coef_start(s, 0)
    for copy in small_copies:
        copy.wait()

    totals = [None] * samples
    mix = list(plan["mix"])
    for turn in range(reduce.depth):
        for s in range(samples):
            totals[s] = coef_sum(s, turn)
            if turn + 1 < reduce.depth:
                coef_start(s, turn + 1)
                work(mix.pop(0) if mix else 0)

    for s in range(samples):
        coef = totals[s][:, :chan]
        grad = totals[s][:, chan:]
        coef_high = coef.astype(BF16).astype(F32)
        grad_high = grad.astype(BF16).astype(F32)
        left_rows[:, s, :] = coef_high
        left_rows[:, samples + s, :] = coef_high
        left_rows[:, 2 * samples + s, :] = coef - coef_high
        right_rows[:, s, :] = grad_high
        right_rows[:, samples + s, :] = grad - grad_high
        right_rows[:, 2 * samples + s, :] = grad_high
    for k in range(owned):
        mixed[k] = dot(right_rows[k].astype(BF16), modes[k], ((1,), (1,)))
    value = jnp.concatenate([mixed[:, s, :] + mixed[:, samples + s, :] for s in range(samples)], axis=1)
    gathered[gather.mine] = value.astype(BF16)

    coef_gather = gather_start(gather, 0, gathered)
    work(chunks)

    columns = plan["columns"]
    rows_each = 2 * chan * columns // size
    wide = hidden_units // columns
    for owner in range(size):
        row = (owner // columns) * rows_each
        source = up_acc if row < chan else down_acc
        row = row % chan
        column = (owner % columns) * wide
        weight_held[0][gather.slot_of(owner)] = source[row:row + rows_each, column:column + wide]
    bias_slots[0][gather.mine[0]] = jnp.sum(bias_acc[...], axis=0, keepdims=True)

    def weights_start(turn):
        at = gather.order[turn]
        slot = bias_slots[turn].at[gather.digits[at]]
        return scatter_start(gather, turn, weight_held, weight_sent, weight_got) + exchange(
            gather, at, [(lambda digit: slot, slot)])

    def weights_sum(turn, copies):
        total = scatter_sum(gather, turn, copies, weight_held, weight_sent, weight_got)
        bias = bias_slots[turn][0]
        for slot in range(1, gather.radices[gather.order[turn]]):
            bias = bias + bias_slots[turn][slot]
        if turn + 1 < gather.depth:
            bias_slots[turn + 1][gather.digits[gather.order[turn + 1]]] = bias
        else:
            grad_bias[...] = bias
            weights_all[gather.mine] = total.astype(BF16)

    weight_copies = weights_start(0)
    for k in range(owned):
        grad_modes[k] = dot(left_rows[k].astype(BF16), right_rows[k].astype(BF16), ((0,), (0,)))
    for turn in range(gather.depth):
        weights_sum(turn, weight_copies)
        if turn + 1 < gather.depth:
            weight_copies = weights_start(turn + 1)
        if turn + 1 == gather.depth:
            weight_copies = gather_start(gather, 0, weights_all)
        finish(coef_gather)
        if turn + 1 < gather.depth:
            coef_gather = gather_start(gather, turn + 1, gathered)

    for owner in range(size):
        natural[owner * owned:(owner + 1) * owned] = gathered[gather.digits_of(owner)]

    def spread(step, carry):
        rows = pl.ds(pl.multiple_of(step * chunk, chunk), chunk)
        value = dot(basis[rows, :], natural[...], ((1,), (0,)))
        for s in range(samples):
            grad_input[s, rows, :] = (value[:, s * chan:(s + 1) * chan] + pointwise[s, rows, :]).astype(BF16)
        return carry

    lax.fori_loop(0, chunks, spread, 0)
    for turn in range(1, gather.depth):
        finish(weight_copies)
        weight_copies = gather_start(gather, turn, weights_all)
    finish(weight_copies)

    for owner in range(size):
        row = (owner // columns) * rows_each
        target = grad_up if row < chan else grad_down
        row = row % chan
        column = (owner % columns) * wide
        target[row:row + rows_each, column:column + wide] = weights_all[gather.digits_of(owner)].astype(F32)


def place_kernel(
    input_from, modes_from, up_from, bias_from, down_from,
    input_to, modes_to, up_to, bias_to, down_to, sems,
):
    copies = (
        pltpu.make_async_copy(input_from, input_to, sems.at[0]),
        pltpu.make_async_copy(modes_from, modes_to, sems.at[1]),
    )
    for copy in copies:
        copy.start()
    up_to[...] = up_from[...]
    bias_to[...] = bias_from[...]
    down_to[...] = down_from[...].T
    for copy in copies:
        copy.wait()


def per_device(size, inputs, cotangent, basis, mode_weights, w_up, b_up, w_down):
    samples, here, chan = inputs.shape
    hidden_units = w_up.shape[1]
    total_modes = basis.shape[1]
    owned = total_modes // size
    reduce, gather = reduce_radices(size), gather_radices(size)
    chunk = min(512, here)
    load_steps = 4
    columns = max(1, min(16 * size // (2 * chan), hidden_units // 256))
    rows_each = 2 * chan * columns // size
    wide = hidden_units // columns
    plan = {
        "size": size, "reduce": reduce, "gather": gather, "chunk": chunk,
        "load_steps": load_steps, "columns": columns, "mix": (1, 2, 2, 1),
    }
    width = 2 * samples * chan
    rows8 = 8 * (-(-3 * samples // 8))
    backwards = tuple(reversed(gather))
    copies = samples * sum(radix - 1 for radix in reduce) + 4 * sum(radix - 1 for radix in gather)
    vmem = pltpu.VMEM
    scratch = [
        vmem((samples, here, chan), BF16),
        vmem((samples, here, chan), BF16),
        vmem((width, here), BF16),
        vmem((here, total_modes), BF16),
        vmem((owned, chan, chan), BF16),
        vmem(w_up.shape, BF16),
        vmem((1, hidden_units), F32),
        vmem(w_down.shape, BF16),
        vmem((width, total_modes), F32),
        vmem((samples, here, chan), F32),
        vmem((chan, hidden_units), F32),
        vmem((chan, hidden_units), F32),
        vmem((8, hidden_units), F32),
        vmem(backwards + (owned, samples * chan), BF16),
        vmem((total_modes, samples * chan), BF16),
        vmem((owned, rows8, chan), F32),
        vmem((owned, rows8, chan), F32),
        vmem((owned, rows8, chan), F32),
        vmem(backwards + (rows_each, wide), BF16),
        pltpu.SemaphoreType.DMA((2 * samples + 5, load_steps)),
        pltpu.SemaphoreType.DMA((copies,)),
        pltpu.SemaphoreType.DMA((copies,)),
    ]

    def stage_buffers(radices, tail, first_type, later_type):
        return [
            vmem(shape + tail, later_type if turn else first_type)
            for turn, shape in enumerate(staged(radices, size))
        ]

    coef_tail, weight_tail = (owned, 2 * chan), (rows_each, wide)
    for first, later in ((F32, F32), (BF16, BF16), (F32, BF16)):
        for _ in range(samples):
            scratch += stage_buffers(reduce, coef_tail, first, later)
    for first, later in ((F32, F32), (BF16, BF16), (F32, BF16)):
        scratch += stage_buffers(gather, weight_tail, first, later)
    scratch += [vmem((shape[0], 1, hidden_units), F32) for shape in staged(gather, size)]
    outside = pl.BlockSpec(memory_space=pltpu.HBM)
    inside = pl.BlockSpec(memory_space=pltpu.VMEM)
    results = pl.pallas_call(
        functools.partial(layer_kernel, plan),
        out_shape=(
            jax.ShapeDtypeStruct((samples, here, chan), BF16),
            jax.ShapeDtypeStruct((owned, chan, chan), F32),
            jax.ShapeDtypeStruct((chan, hidden_units), F32),
            jax.ShapeDtypeStruct((1, hidden_units), F32),
            jax.ShapeDtypeStruct((chan, hidden_units), F32),
        ),
        in_specs=[outside] * 7,
        out_specs=(inside,) * 5,
        scratch_shapes=scratch,
        compiler_params=pltpu.CompilerParams(
            collective_id=0, has_side_effects=True, vmem_limit_bytes=44 * 1024 * 1024
        ),
        name="layer",
    )(*(pltpu.with_memory_space_constraint(x, pltpu.HBM) for x in (
        inputs, cotangent, basis, mode_weights, w_up, b_up.reshape(1, hidden_units), w_down)))
    grad_input, grad_modes, grad_up, grad_bias, grad_down = pl.pallas_call(
        place_kernel,
        out_shape=(
            jax.ShapeDtypeStruct((samples, here, chan), BF16),
            jax.ShapeDtypeStruct((owned, chan, chan), F32),
            jax.ShapeDtypeStruct((chan, hidden_units), F32),
            jax.ShapeDtypeStruct((1, hidden_units), F32),
            jax.ShapeDtypeStruct((hidden_units, chan), F32),
        ),
        in_specs=[inside] * 5,
        out_specs=(outside, outside, inside, inside, inside),
        scratch_shapes=[pltpu.SemaphoreType.DMA((2,))],
        compiler_params=pltpu.CompilerParams(vmem_limit_bytes=8 * 1024 * 1024),
        name="place",
    )(*results)
    return grad_input, grad_modes, grad_up, grad_bias.reshape(hidden_units), grad_down


def solution(mesh):
    size = mesh.shape["vert"]
    groups = mesh.shape["samp"]

    def body(*arguments):
        grad_input, grad_modes, grad_up, grad_bias, grad_down = per_device(size, *arguments)
        if groups > 1:
            grad_modes, grad_up, grad_bias, grad_down = lax.psum(
                (grad_modes, grad_up, grad_bias, grad_down), "samp"
            )
        return grad_input, grad_modes, grad_up, grad_bias, grad_down

    in_specs = (
        P("samp", "vert", None),
        P("samp", "vert", None),
        P("vert", None),
        P("vert", None, None),
        P(),
        P(),
        P(),
    )
    out_specs = (P("samp", "vert", None), P("vert", None, None), P(), P(), P())
    return jax.shard_map(body, mesh=mesh, in_specs=in_specs, out_specs=out_specs, check_vma=False)
```

```python
import functools

import jax
import jax.numpy as jnp
from jax import lax
from jax.experimental import pallas as pl
from jax.experimental.pallas import tpu as pltpu
from jax.sharding import PartitionSpec as P

F32 = jnp.float32
BF16 = jnp.bfloat16
MESH = pl.DeviceIdType.MESH
ROOT = 0.7978845608
CUBE = 0.044715


def reduce_radices(size):
    return (size // 8, 4, 2) if size % 16 == 0 else gather_radices(size)


def gather_radices(size):
    return (size // 2, 2) if size % 4 == 0 else (size,)


def staged(radices, size):
    left, found = size, []
    for radix in reversed(radices):
        left //= radix
        found.append((radix, left))
    return found


def dot(left, right, contract):
    return lax.dot_general(left, right, (contract, ((), ())), preferred_element_type=F32)


class Grid:
    def __init__(self, me, radices):
        self.me, self.radices, self.depth = me, radices, len(radices)
        self.strides = [1] * self.depth
        for at in range(self.depth - 2, -1, -1):
            self.strides[at] = self.strides[at + 1] * radices[at + 1]
        self.digits = [lax.rem(lax.div(me, self.strides[at]), radices[at]) for at in range(self.depth)]
        self.order = tuple(reversed(range(self.depth)))
        self.mine = tuple(self.digits[at] for at in self.order)

    def peer(self, at, shift):
        digit = lax.rem(self.digits[at] + shift, self.radices[at])
        return digit, {"vert": self.me + (digit - self.digits[at]) * self.strides[at]}

    def digits_of(self, owner):
        return tuple((owner // self.strides[at]) % self.radices[at] for at in self.order)

    def slot_of(self, owner):
        found = self.digits_of(owner)
        rest, scale = 0, 1
        for at, digit in zip(self.order[1:], found[1:]):
            rest += digit * scale
            scale *= self.radices[at]
        return found[0], rest


def layer_kernel(
    plan,
    inputs_hbm, cotangent_hbm, basis_hbm, modes_hbm, w_up_hbm, b_up_hbm, w_down_hbm,
    grad_input, grad_modes, grad_up, grad_bias, grad_down,
    xs, cs, xt, basis, modes, w_up, b_up, w_down, w_half, b_half, acc, pointwise,
    up_acc, down_acc, bias_acc, gathered, natural, left_rows, right_rows, mixed,
    weights_all, in_sems, send_sems, recv_sems, *stages,
):
    size = plan["size"]
    samples, here, chan = xs.shape
    hidden_units = w_up.shape[1]
    total_modes = basis.shape[1]
    owned = total_modes // size
    me = lax.axis_index("vert")
    reduce, gather = Grid(me, plan["reduce"]), Grid(me, plan["gather"])
    pool = list(stages)

    def take(count):
        found = pool[:count]
        del pool[:count]
        return found

    coef_held = [take(reduce.depth) for _ in range(samples)]
    coef_sent = [take(reduce.depth) for _ in range(samples)]
    coef_got = [take(reduce.depth) for _ in range(samples)]
    weight_held, weight_sent, weight_got = take(gather.depth), take(gather.depth), take(gather.depth)
    bias_slots = take(gather.depth)

    load_steps = plan["load_steps"]
    load_rows = here // load_steps

    def row_block(step):
        return pl.ds(pl.multiple_of(step * load_rows, load_rows), load_rows)

    def field_loads(s, step):
        rows = row_block(step)
        return (
            pltpu.make_async_copy(inputs_hbm.at[s, rows], xs.at[s, rows], in_sems.at[2 * s, step]),
            pltpu.make_async_copy(cotangent_hbm.at[s, rows], cs.at[s, rows], in_sems.at[2 * s + 1, step]),
        )

    def basis_load(step):
        rows = row_block(step)
        return pltpu.make_async_copy(basis_hbm.at[rows], basis.at[rows], in_sems.at[2 * samples, step])

    small_copies = [
        pltpu.make_async_copy(source, target, in_sems.at[2 * samples + 1 + at, 0])
        for at, (source, target) in enumerate(
            ((w_up_hbm, w_up), (b_up_hbm, b_up), (w_down_hbm, w_down), (modes_hbm, modes)))
    ]
    for step in range(load_steps):
        for copy in field_loads(0, step):
            copy.start()
        basis_load(step).start()
    for s in range(1, samples):
        for step in range(load_steps):
            for copy in field_loads(s, step):
                copy.start()
    for copy in small_copies:
        copy.start()

    barrier = pltpu.get_barrier_semaphore()
    peers = 0
    for at in range(gather.depth):
        for shift in range(1, gather.radices[at]):
            pl.semaphore_signal(barrier, inc=1, device_id=gather.peer(at, shift)[1], device_id_type=MESH)
            peers += 1

    acc[...] = jnp.zeros_like(acc)
    up_acc[...] = jnp.zeros_like(up_acc)
    down_acc[...] = jnp.zeros_like(down_acc)
    bias_acc[...] = jnp.zeros_like(bias_acc)
    left_rows[...] = jnp.zeros_like(left_rows)
    right_rows[...] = jnp.zeros_like(right_rows)

    sem_at = [0]

    def exchange(grid, at, pairs):
        copies = []
        for shift in range(1, grid.radices[at]):
            digit, target = grid.peer(at, shift)
            for source_of, dest in pairs:
                copies.append(pltpu.make_async_remote_copy(
                    src_ref=source_of(digit),
                    dst_ref=dest,
                    send_sem=send_sems.at[sem_at[0]],
                    recv_sem=recv_sems.at[sem_at[0]],
                    device_id=target,
                    device_id_type=MESH,
                ))
                sem_at[0] += 1
        for copy in copies:
            copy.start()
        return copies

    def finish(copies):
        for copy in copies:
            copy.wait()

    def scatter_start(grid, turn, held, sent, got):
        at = grid.order[turn]
        source = (held if turn == 0 else sent)[turn]
        return exchange(grid, at, [(lambda digit: source.at[digit], got[turn].at[grid.digits[at]])])

    def scatter_sum(grid, turn, copies, held, sent, got):
        finish(copies)
        at = grid.order[turn]
        for block in range(held[turn].shape[1]):
            value = held[turn][grid.digits[at], block]
            for shift in range(1, grid.radices[at]):
                value = value + got[turn][grid.peer(at, shift)[0], block].astype(F32)
            if turn + 1 == grid.depth:
                return value
            radix = grid.radices[grid.order[turn + 1]]
            held[turn + 1][block % radix, block // radix] = value
            sent[turn + 1][block % radix, block // radix] = value.astype(BF16)

    def gather_start(grid, turn, ref):
        held = ref.at[grid.mine[:grid.depth - turn]]
        return exchange(grid, grid.order[grid.depth - 1 - turn], [(lambda digit: held, held)])

    chunk = plan["chunk"]
    chunks = here // chunk
    done_chunks = [0]

    def point(step, carry):
        rows = pl.ds(pl.multiple_of(step * chunk, chunk), chunk)
        ones = jnp.ones((8, chunk), BF16)
        for s in range(samples):
            middle = dot(xs[s, rows, :], w_half[...], ((1,), (0,))) + b_half[...]
            square = middle * middle
            t = jnp.tanh(middle * (2.0 * ROOT + (8.0 * ROOT * CUBE) * square))
            plus = 1.0 + t
            hidden = (middle * plus).astype(BF16)
            slope = plus * (0.5 + middle * (1.0 - t) * (ROOT + (12.0 * ROOT * CUBE) * square))
            grad_hidden = dot(cs[s, rows, :], w_down[...], ((1,), (1,)))
            grad_pre = (grad_hidden * slope).astype(BF16)
            pointwise[s, rows, :] = dot(grad_pre, w_up[...], ((1,), (1,)))
            up_acc[...] += dot(xt[2 * s * chan:(2 * s + 1) * chan, rows], grad_pre, ((1,), (0,)))
            down_acc[...] += dot(xt[(2 * s + 1) * chan:(2 * s + 2) * chan, rows], hidden, ((1,), (0,)))
            bias_acc[...] += dot(ones, grad_pre, ((1,), (0,)))
        return carry

    def work(count):
        first = done_chunks[0]
        last = min(chunks, first + count)
        done_chunks[0] = last
        if last > first:
            lax.fori_loop(first, last, point, 0)

    coef_copies = [None] * samples

    def coef_start(s, turn):
        coef_copies[s] = scatter_start(reduce, turn, coef_held[s], coef_sent[s], coef_got[s])

    def coef_sum(s, turn):
        return scatter_sum(reduce, turn, coef_copies[s], coef_held[s], coef_sent[s], coef_got[s])

    for s in range(samples):
        def project(step, carry):
            if s == 0:
                basis_load(step).wait()
            for copy in field_loads(s, step):
                copy.wait()
            rows = row_block(step)
            low = 2 * s * chan
            xt[low:low + chan, rows] = xs[s, rows, :].T
            xt[low + chan:low + 2 * chan, rows] = cs[s, rows, :].T
            acc[low:low + 2 * chan] += dot(xt[low:low + 2 * chan, rows], basis[rows, :], ((1,), (0,)))
            return carry

        lax.fori_loop(0, load_steps, project, 0)
        if s == 0:
            pl.semaphore_wait(barrier, peers)
        for block in range(total_modes // 128):
            tile = acc[2 * s * chan:2 * (s + 1) * chan, block * 128:(block + 1) * 128].T
            for part in range(128 // owned):
                owner = block * (128 // owned) + part
                coef_held[s][0][reduce.slot_of(owner)] = tile[part * owned:(part + 1) * owned]
        coef_start(s, 0)
    for copy in small_copies:
        copy.wait()
    w_half[...] = w_up[...] * jnp.bfloat16(0.5)
    b_half[...] = b_up[...] * 0.5

    totals = [None] * samples
    mix = list(plan["mix"])
    for turn in range(reduce.depth):
        for s in range(samples):
            totals[s] = coef_sum(s, turn)
            if turn + 1 < reduce.depth:
                coef_start(s, turn + 1)
                work(mix.pop(0) if mix else 0)

    for s in range(samples):
        coef = totals[s][:, :chan]
        grad = totals[s][:, chan:]
        coef_high = coef.astype(BF16).astype(F32)
        grad_high = grad.astype(BF16).astype(F32)
        left_rows[:, s, :] = coef_high
        left_rows[:, samples + s, :] = coef_high
        left_rows[:, 2 * samples + s, :] = coef - coef_high
        right_rows[:, s, :] = grad_high
        right_rows[:, samples + s, :] = grad - grad_high
        right_rows[:, 2 * samples + s, :] = grad_high
    for k in range(owned):
        mixed[k] = dot(right_rows[k].astype(BF16), modes[k], ((1,), (1,)))
    value = jnp.concatenate([mixed[:, s, :] + mixed[:, samples + s, :] for s in range(samples)], axis=1)
    gathered[gather.mine] = value.astype(BF16)

    coef_gather = gather_start(gather, 0, gathered)
    work(chunks)

    columns = plan["columns"]
    rows_each = 2 * chan * columns // size
    wide = hidden_units // columns
    for owner in range(size):
        row = (owner // columns) * rows_each
        source = up_acc if row < chan else down_acc
        row = row % chan
        column = (owner % columns) * wide
        weight_held[0][gather.slot_of(owner)] = source[row:row + rows_each, column:column + wide]
    bias_slots[0][gather.mine[0]] = bias_acc[0:1]

    def weights_start(turn):
        at = gather.order[turn]
        slot = bias_slots[turn].at[gather.digits[at]]
        return scatter_start(gather, turn, weight_held, weight_sent, weight_got) + exchange(
            gather, at, [(lambda digit: slot, slot)])

    def weights_sum(turn, copies):
        total = scatter_sum(gather, turn, copies, weight_held, weight_sent, weight_got)
        bias = bias_slots[turn][0]
        for slot in range(1, gather.radices[gather.order[turn]]):
            bias = bias + bias_slots[turn][slot]
        if turn + 1 < gather.depth:
            bias_slots[turn + 1][gather.digits[gather.order[turn + 1]]] = bias
        else:
            grad_bias[...] = bias
            weights_all[gather.mine] = total.astype(BF16)

    weight_copies = weights_start(0)
    for k in range(owned):
        grad_modes[k] = dot(left_rows[k].astype(BF16), right_rows[k].astype(BF16), ((0,), (0,)))
    for turn in range(gather.depth):
        weights_sum(turn, weight_copies)
        if turn + 1 < gather.depth:
            weight_copies = weights_start(turn + 1)
        if turn + 1 == gather.depth:
            weight_copies = gather_start(gather, 0, weights_all)
        finish(coef_gather)
        if turn + 1 < gather.depth:
            coef_gather = gather_start(gather, turn + 1, gathered)

    for owner in range(size):
        natural[owner * owned:(owner + 1) * owned] = gathered[gather.digits_of(owner)]

    def spread(step, carry):
        rows = pl.ds(pl.multiple_of(step * chunk, chunk), chunk)
        value = dot(basis[rows, :], natural[...], ((1,), (0,)))
        for s in range(samples):
            grad_input[s, rows, :] = (value[:, s * chan:(s + 1) * chan] + pointwise[s, rows, :]).astype(BF16)
        return carry

    lax.fori_loop(0, chunks, spread, 0)
    for turn in range(1, gather.depth):
        finish(weight_copies)
        weight_copies = gather_start(gather, turn, weights_all)
    finish(weight_copies)

    for owner in range(size):
        row = (owner // columns) * rows_each
        target = grad_up if row < chan else grad_down
        row = row % chan
        column = (owner % columns) * wide
        target[row:row + rows_each, column:column + wide] = weights_all[gather.digits_of(owner)].astype(F32)


def place_kernel(
    input_from, modes_from, up_from, bias_from, down_from,
    input_to, modes_to, up_to, bias_to, down_to, turned, sems,
):
    pairs = []
    for source, target, parts in ((input_from, input_to, 2), (modes_from, modes_to, 2)):
        rows = source.shape[-2 if source is input_from else 0] // parts
        for part in range(parts):
            here = pl.ds(part * rows, rows)
            where = (slice(None), here) if source is input_from else (here,)
            pairs.append((source.at[where], target.at[where]))
    pairs += [(up_from, up_to), (bias_from, bias_to), (turned, down_to)]
    copies = [pltpu.make_async_copy(*pair, sems.at[at]) for at, pair in enumerate(pairs)]
    for copy in copies[:-1]:
        copy.start()
    turned[...] = down_from[...].T
    copies[-1].start()
    for copy in copies:
        copy.wait()


def per_device(size, inputs, cotangent, basis, mode_weights, w_up, b_up, w_down):
    samples, here, chan = inputs.shape
    hidden_units = w_up.shape[1]
    total_modes = basis.shape[1]
    owned = total_modes // size
    reduce, gather = reduce_radices(size), gather_radices(size)
    chunk = min(512, here)
    load_steps = 4
    columns = max(1, min(16 * size // (2 * chan), hidden_units // 256))
    rows_each = 2 * chan * columns // size
    wide = hidden_units // columns
    plan = {
        "size": size, "reduce": reduce, "gather": gather, "chunk": chunk,
        "load_steps": load_steps, "columns": columns, "mix": (1, 2, 1, 1),
    }
    width = 2 * samples * chan
    rows8 = 8 * (-(-3 * samples // 8))
    backwards = tuple(reversed(gather))
    copies = samples * sum(radix - 1 for radix in reduce) + 4 * sum(radix - 1 for radix in gather)
    vmem = pltpu.VMEM
    scratch = [
        vmem((samples, here, chan), BF16),
        vmem((samples, here, chan), BF16),
        vmem((width, here), BF16),
        vmem((here, total_modes), BF16),
        vmem((owned, chan, chan), BF16),
        vmem(w_up.shape, BF16),
        vmem((1, hidden_units), F32),
        vmem(w_down.shape, BF16),
        vmem(w_up.shape, BF16),
        vmem((1, hidden_units), F32),
        vmem((width, total_modes), F32),
        vmem((samples, here, chan), F32),
        vmem((chan, hidden_units), F32),
        vmem((chan, hidden_units), F32),
        vmem((8, hidden_units), F32),
        vmem(backwards + (owned, samples * chan), BF16),
        vmem((total_modes, samples * chan), BF16),
        vmem((owned, rows8, chan), F32),
        vmem((owned, rows8, chan), F32),
        vmem((owned, rows8, chan), F32),
        vmem(backwards + (rows_each, wide), BF16),
        pltpu.SemaphoreType.DMA((2 * samples + 5, load_steps)),
        pltpu.SemaphoreType.DMA((copies,)),
        pltpu.SemaphoreType.DMA((copies,)),
    ]

    def stage_buffers(radices, tail, first_type, later_type):
        return [
            vmem(shape + tail, later_type if turn else first_type)
            for turn, shape in enumerate(staged(radices, size))
        ]

    coef_tail, weight_tail = (owned, 2 * chan), (rows_each, wide)
    for first, later in ((F32, F32), (BF16, BF16), (F32, BF16)):
        for _ in range(samples):
            scratch += stage_buffers(reduce, coef_tail, first, later)
    for first, later in ((F32, F32), (BF16, BF16), (F32, BF16)):
        scratch += stage_buffers(gather, weight_tail, first, later)
    scratch += [vmem((shape[0], 1, hidden_units), F32) for shape in staged(gather, size)]
    outside = pl.BlockSpec(memory_space=pltpu.HBM)
    inside = pl.BlockSpec(memory_space=pltpu.VMEM)
    results = pl.pallas_call(
        functools.partial(layer_kernel, plan),
        out_shape=(
            jax.ShapeDtypeStruct((samples, here, chan), BF16),
            jax.ShapeDtypeStruct((owned, chan, chan), F32),
            jax.ShapeDtypeStruct((chan, hidden_units), F32),
            jax.ShapeDtypeStruct((1, hidden_units), F32),
            jax.ShapeDtypeStruct((chan, hidden_units), F32),
        ),
        in_specs=[outside] * 7,
        out_specs=(inside,) * 5,
        scratch_shapes=scratch,
        compiler_params=pltpu.CompilerParams(
            collective_id=0, has_side_effects=True, vmem_limit_bytes=45 * 1024 * 1024
        ),
        name="layer",
    )(*(pltpu.with_memory_space_constraint(x, pltpu.HBM) for x in (
        inputs, cotangent, basis, mode_weights, w_up, b_up.reshape(1, hidden_units), w_down)))
    grad_input, grad_modes, grad_up, grad_bias, grad_down = pl.pallas_call(
        place_kernel,
        out_shape=(
            jax.ShapeDtypeStruct((samples, here, chan), BF16),
            jax.ShapeDtypeStruct((owned, chan, chan), F32),
            jax.ShapeDtypeStruct((chan, hidden_units), F32),
            jax.ShapeDtypeStruct((1, hidden_units), F32),
            jax.ShapeDtypeStruct((hidden_units, chan), F32),
        ),
        in_specs=[inside] * 5,
        out_specs=(outside,) * 5,
        scratch_shapes=[vmem((hidden_units, chan), F32), pltpu.SemaphoreType.DMA((2 * 2 + 3,))],
        compiler_params=pltpu.CompilerParams(vmem_limit_bytes=8 * 1024 * 1024),
        name="place",
    )(*results)
    return grad_input, grad_modes, grad_up, grad_bias.reshape(hidden_units), grad_down


def solution(mesh):
    size = mesh.shape["vert"]
    groups = mesh.shape["samp"]

    def body(*arguments):
        grad_input, grad_modes, grad_up, grad_bias, grad_down = per_device(size, *arguments)
        if groups > 1:
            grad_modes, grad_up, grad_bias, grad_down = lax.psum(
                (grad_modes, grad_up, grad_bias, grad_down), "samp"
            )
        return grad_input, grad_modes, grad_up, grad_bias, grad_down

    in_specs = (
        P("samp", "vert", None),
        P("samp", "vert", None),
        P("vert", None),
        P("vert", None, None),
        P(),
        P(),
        P(),
    )
    out_specs = (P("samp", "vert", None), P("vert", None, None), P(), P(), P())
    return jax.shard_map(body, mesh=mesh, in_specs=in_specs, out_specs=out_specs, check_vma=False)
```

```python
import functools

import jax
import jax.numpy as jnp
from jax import lax
from jax.experimental import pallas as pl
from jax.experimental.pallas import tpu as pltpu
from jax.sharding import PartitionSpec as P

F32 = jnp.float32
BF16 = jnp.bfloat16
MESH = pl.DeviceIdType.MESH
ROOT = 0.7978845608
CUBE = 0.044715


def reduce_radices(size):
    return (size // 8, 4, 2) if size % 16 == 0 else gather_radices(size)


def gather_radices(size):
    return (size // 2, 2) if size % 4 == 0 else (size,)


def staged(radices, size):
    left, found = size, []
    for radix in reversed(radices):
        left //= radix
        found.append((radix, left))
    return found


def dot(left, right, contract):
    return lax.dot_general(left, right, (contract, ((), ())), preferred_element_type=F32)


class Grid:
    def __init__(self, me, radices):
        self.me, self.radices, self.depth = me, radices, len(radices)
        self.strides = [1] * self.depth
        for at in range(self.depth - 2, -1, -1):
            self.strides[at] = self.strides[at + 1] * radices[at + 1]
        self.digits = [lax.rem(lax.div(me, self.strides[at]), radices[at]) for at in range(self.depth)]
        self.order = tuple(reversed(range(self.depth)))
        self.mine = tuple(self.digits[at] for at in self.order)

    def peer(self, at, shift):
        digit = lax.rem(self.digits[at] + shift, self.radices[at])
        return digit, {"vert": self.me + (digit - self.digits[at]) * self.strides[at]}

    def digits_of(self, owner):
        return tuple((owner // self.strides[at]) % self.radices[at] for at in self.order)

    def slot_of(self, owner):
        found = self.digits_of(owner)
        rest, scale = 0, 1
        for at, digit in zip(self.order[1:], found[1:]):
            rest += digit * scale
            scale *= self.radices[at]
        return found[0], rest


def layer_kernel(
    plan,
    inputs_hbm, cotangent_hbm, basis_hbm, modes_hbm, w_up_hbm, b_up_hbm, w_down_hbm,
    grad_input, grad_modes, grad_up, grad_bias, grad_down,
    xs, cs, xt, basis, modes, w_up, b_up, w_down, w_half, b_half, acc, pointwise,
    up_acc, down_acc, bias_acc, gathered, natural, left_rows, right_rows, mixed,
    weights_all, in_sems, send_sems, recv_sems, *stages,
):
    size = plan["size"]
    samples, here, chan = xs.shape
    hidden_units = w_up.shape[1]
    total_modes = basis.shape[1]
    owned = total_modes // size
    me = lax.axis_index("vert")
    reduce, gather = Grid(me, plan["reduce"]), Grid(me, plan["gather"])
    pool = list(stages)

    def take(count):
        found = pool[:count]
        del pool[:count]
        return found

    coef_held = [take(reduce.depth) for _ in range(samples)]
    coef_sent = [take(reduce.depth) for _ in range(samples)]
    coef_got = [take(reduce.depth) for _ in range(samples)]
    weight_held, weight_sent, weight_got = take(gather.depth), take(gather.depth), take(gather.depth)
    bias_slots = take(gather.depth)

    load_steps = plan["load_steps"]
    load_rows = here // load_steps

    def row_block(step):
        return pl.ds(pl.multiple_of(step * load_rows, load_rows), load_rows)

    def field_loads(s, step):
        rows = row_block(step)
        return (
            pltpu.make_async_copy(inputs_hbm.at[s, rows], xs.at[s, rows], in_sems.at[2 * s, step]),
            pltpu.make_async_copy(cotangent_hbm.at[s, rows], cs.at[s, rows], in_sems.at[2 * s + 1, step]),
        )

    def basis_load(step):
        rows = row_block(step)
        return pltpu.make_async_copy(basis_hbm.at[rows], basis.at[rows], in_sems.at[2 * samples, step])

    small_copies = [
        pltpu.make_async_copy(source, target, in_sems.at[2 * samples + 1 + at, 0])
        for at, (source, target) in enumerate(
            ((w_up_hbm, w_up), (b_up_hbm, b_up), (w_down_hbm, w_down), (modes_hbm, modes)))
    ]
    for step in range(load_steps):
        for copy in field_loads(0, step):
            copy.start()
        basis_load(step).start()
    for s in range(1, samples):
        for step in range(load_steps):
            for copy in field_loads(s, step):
                copy.start()
    for copy in small_copies:
        copy.start()

    barrier = pltpu.get_barrier_semaphore()
    peers = 0
    for at in range(gather.depth):
        for shift in range(1, gather.radices[at]):
            pl.semaphore_signal(barrier, inc=1, device_id=gather.peer(at, shift)[1], device_id_type=MESH)
            peers += 1

    acc[...] = jnp.zeros_like(acc)
    up_acc[...] = jnp.zeros_like(up_acc)
    down_acc[...] = jnp.zeros_like(down_acc)
    bias_acc[...] = jnp.zeros_like(bias_acc)
    left_rows[...] = jnp.zeros_like(left_rows)
    right_rows[...] = jnp.zeros_like(right_rows)

    sem_at = [0]

    def exchange(grid, at, pairs):
        copies = []
        for shift in range(1, grid.radices[at]):
            digit, target = grid.peer(at, shift)
            for source_of, dest in pairs:
                copies.append(pltpu.make_async_remote_copy(
                    src_ref=source_of(digit),
                    dst_ref=dest,
                    send_sem=send_sems.at[sem_at[0]],
                    recv_sem=recv_sems.at[sem_at[0]],
                    device_id=target,
                    device_id_type=MESH,
                ))
                sem_at[0] += 1
        for copy in copies:
            copy.start()
        return copies

    def finish(copies):
        for copy in copies:
            copy.wait()

    def scatter_start(grid, turn, held, sent, got):
        at = grid.order[turn]
        source = (held if turn == 0 else sent)[turn]
        return exchange(grid, at, [(lambda digit: source.at[digit], got[turn].at[grid.digits[at]])])

    def scatter_sum(grid, turn, copies, held, sent, got):
        finish(copies)
        at = grid.order[turn]
        for block in range(held[turn].shape[1]):
            value = held[turn][grid.digits[at], block]
            for shift in range(1, grid.radices[at]):
                value = value + got[turn][grid.peer(at, shift)[0], block].astype(F32)
            if turn + 1 == grid.depth:
                return value
            radix = grid.radices[grid.order[turn + 1]]
            held[turn + 1][block % radix, block // radix] = value
            sent[turn + 1][block % radix, block // radix] = value.astype(BF16)

    def gather_start(grid, turn, ref):
        held = ref.at[grid.mine[:grid.depth - turn]]
        return exchange(grid, grid.order[grid.depth - 1 - turn], [(lambda digit: held, held)])

    chunk = plan["chunk"]
    chunks = here // chunk
    done_chunks = [0]

    def point(step, carry):
        rows = pl.ds(pl.multiple_of(step * chunk, chunk), chunk)
        ones = jnp.ones((8, chunk), BF16)
        for s in range(samples):
            middle = dot(xs[s, rows, :], w_half[...], ((1,), (0,))) + b_half[...]
            square = middle * middle
            t = jnp.tanh(middle * (2.0 * ROOT + (8.0 * ROOT * CUBE) * square))
            plus = 1.0 + t
            hidden = (middle * plus).astype(BF16)
            slope = plus * (0.5 + middle * (1.0 - t) * (ROOT + (12.0 * ROOT * CUBE) * square))
            grad_hidden = dot(cs[s, rows, :], w_down[...], ((1,), (1,)))
            grad_pre = (grad_hidden * slope).astype(BF16)
            pointwise[s, rows, :] = dot(grad_pre, w_up[...], ((1,), (1,)))
            up_acc[...] += dot(xt[2 * s * chan:(2 * s + 1) * chan, rows], grad_pre, ((1,), (0,)))
            down_acc[...] += dot(xt[(2 * s + 1) * chan:(2 * s + 2) * chan, rows], hidden, ((1,), (0,)))
            bias_acc[...] += dot(ones, grad_pre, ((1,), (0,)))
        return carry

    def work(count):
        first = done_chunks[0]
        last = min(chunks, first + count)
        done_chunks[0] = last
        if last > first:
            lax.fori_loop(first, last, point, 0)

    coef_copies = [None] * samples

    def coef_start(s, turn):
        coef_copies[s] = scatter_start(reduce, turn, coef_held[s], coef_sent[s], coef_got[s])

    def coef_sum(s, turn):
        return scatter_sum(reduce, turn, coef_copies[s], coef_held[s], coef_sent[s], coef_got[s])

    for s in range(samples):
        def project(step, carry):
            if s == 0:
                basis_load(step).wait()
            for copy in field_loads(s, step):
                copy.wait()
            rows = row_block(step)
            low = 2 * s * chan
            xt[low:low + chan, rows] = xs[s, rows, :].T
            xt[low + chan:low + 2 * chan, rows] = cs[s, rows, :].T
            acc[low:low + 2 * chan] += dot(xt[low:low + 2 * chan, rows], basis[rows, :], ((1,), (0,)))
            return carry

        lax.fori_loop(0, load_steps, project, 0)
        if s == 0:
            pl.semaphore_wait(barrier, peers)
        for block in range(total_modes // 128):
            tile = acc[2 * s * chan:2 * (s + 1) * chan, block * 128:(block + 1) * 128].T
            for part in range(128 // owned):
                owner = block * (128 // owned) + part
                coef_held[s][0][reduce.slot_of(owner)] = tile[part * owned:(part + 1) * owned]
        coef_start(s, 0)
    for copy in small_copies:
        copy.wait()
    w_half[...] = w_up[...] * jnp.bfloat16(0.5)
    b_half[...] = b_up[...] * 0.5

    totals = [None] * samples
    mix = list(plan["mix"])
    for turn in range(reduce.depth):
        for s in range(samples):
            totals[s] = coef_sum(s, turn)
            if turn + 1 < reduce.depth:
                coef_start(s, turn + 1)
                work(mix.pop(0) if mix else 0)

    for s in range(samples):
        coef = totals[s][:, :chan]
        grad = totals[s][:, chan:]
        coef_high = coef.astype(BF16).astype(F32)
        grad_high = grad.astype(BF16).astype(F32)
        left_rows[:, s, :] = coef_high
        left_rows[:, samples + s, :] = coef_high
        left_rows[:, 2 * samples + s, :] = coef - coef_high
        right_rows[:, s, :] = grad_high
        right_rows[:, samples + s, :] = grad - grad_high
        right_rows[:, 2 * samples + s, :] = grad_high
    for k in range(owned):
        mixed[k] = dot(right_rows[k].astype(BF16), modes[k], ((1,), (1,)))
    value = jnp.concatenate([mixed[:, s, :] + mixed[:, samples + s, :] for s in range(samples)], axis=1)
    gathered[gather.mine] = value.astype(BF16)

    coef_gather = gather_start(gather, 0, gathered)
    work(chunks)

    columns = plan["columns"]
    rows_each = 2 * chan * columns // size
    wide = hidden_units // columns
    for owner in range(size):
        row = (owner // columns) * rows_each
        source = up_acc if row < chan else down_acc
        row = row % chan
        column = (owner % columns) * wide
        weight_held[0][gather.slot_of(owner)] = source[row:row + rows_each, column:column + wide]
    bias_slots[0][gather.mine[0]] = bias_acc[0:1]

    def weights_start(turn):
        at = gather.order[turn]
        slot = bias_slots[turn].at[gather.digits[at]]
        return scatter_start(gather, turn, weight_held, weight_sent, weight_got) + exchange(
            gather, at, [(lambda digit: slot, slot)])

    def weights_sum(turn, copies):
        total = scatter_sum(gather, turn, copies, weight_held, weight_sent, weight_got)
        bias = bias_slots[turn][0]
        for slot in range(1, gather.radices[gather.order[turn]]):
            bias = bias + bias_slots[turn][slot]
        if turn + 1 < gather.depth:
            bias_slots[turn + 1][gather.digits[gather.order[turn + 1]]] = bias
        else:
            grad_bias[...] = bias
            weights_all[gather.mine] = total.astype(BF16)

    weight_copies = weights_start(0)
    for turn in range(gather.depth):
        weights_sum(turn, weight_copies)
        if turn + 1 < gather.depth:
            weight_copies = weights_start(turn + 1)
        if turn == 0:
            for k in range(owned):
                grad_modes[k] = dot(left_rows[k].astype(BF16), right_rows[k].astype(BF16), ((0,), (0,)))
        if turn + 1 == gather.depth:
            weight_copies = gather_start(gather, 0, weights_all)
        finish(coef_gather)
        if turn + 1 < gather.depth:
            coef_gather = gather_start(gather, turn + 1, gathered)

    for owner in range(size):
        natural[owner * owned:(owner + 1) * owned] = gathered[gather.digits_of(owner)]

    def spread(step, carry):
        rows = pl.ds(pl.multiple_of(step * chunk, chunk), chunk)
        value = dot(basis[rows, :], natural[...], ((1,), (0,)))
        for s in range(samples):
            grad_input[s, rows, :] = (value[:, s * chan:(s + 1) * chan] + pointwise[s, rows, :]).astype(BF16)
        return carry

    lax.fori_loop(0, chunks, spread, 0)
    for turn in range(1, gather.depth):
        finish(weight_copies)
        weight_copies = gather_start(gather, turn, weights_all)
    finish(weight_copies)

    for owner in range(size):
        row = (owner // columns) * rows_each
        target = grad_up if row < chan else grad_down
        row = row % chan
        column = (owner % columns) * wide
        target[row:row + rows_each, column:column + wide] = weights_all[gather.digits_of(owner)].astype(F32)


def place_kernel(
    input_from, modes_from, up_from, bias_from, down_from,
    input_to, modes_to, up_to, bias_to, down_to, turned, sems,
):
    pairs = []
    for source, target, parts in ((input_from, input_to, 2), (modes_from, modes_to, 2)):
        rows = source.shape[-2 if source is input_from else 0] // parts
        for part in range(parts):
            here = pl.ds(part * rows, rows)
            where = (slice(None), here) if source is input_from else (here,)
            pairs.append((source.at[where], target.at[where]))
    pairs += [(up_from, up_to), (bias_from, bias_to), (turned, down_to)]
    copies = [pltpu.make_async_copy(*pair, sems.at[at]) for at, pair in enumerate(pairs)]
    for copy in copies[:-1]:
        copy.start()
    turned[...] = down_from[...].T
    copies[-1].start()
    for copy in copies:
        copy.wait()


def per_device(size, inputs, cotangent, basis, mode_weights, w_up, b_up, w_down):
    samples, here, chan = inputs.shape
    hidden_units = w_up.shape[1]
    total_modes = basis.shape[1]
    owned = total_modes // size
    reduce, gather = reduce_radices(size), gather_radices(size)
    chunk = min(512, here)
    load_steps = 4
    columns = max(1, min(16 * size // (2 * chan), hidden_units // 256))
    rows_each = 2 * chan * columns // size
    wide = hidden_units // columns
    plan = {
        "size": size, "reduce": reduce, "gather": gather, "chunk": chunk,
        "load_steps": load_steps, "columns": columns, "mix": (1, 2, 1, 1),
    }
    width = 2 * samples * chan
    rows8 = 8 * (-(-3 * samples // 8))
    backwards = tuple(reversed(gather))
    copies = samples * sum(radix - 1 for radix in reduce) + 4 * sum(radix - 1 for radix in gather)
    vmem = pltpu.VMEM
    scratch = [
        vmem((samples, here, chan), BF16),
        vmem((samples, here, chan), BF16),
        vmem((width, here), BF16),
        vmem((here, total_modes), BF16),
        vmem((owned, chan, chan), BF16),
        vmem(w_up.shape, BF16),
        vmem((1, hidden_units), F32),
        vmem(w_down.shape, BF16),
        vmem(w_up.shape, BF16),
        vmem((1, hidden_units), F32),
        vmem((width, total_modes), F32),
        vmem((samples, here, chan), F32),
        vmem((chan, hidden_units), F32),
        vmem((chan, hidden_units), F32),
        vmem((8, hidden_units), F32),
        vmem(backwards + (owned, samples * chan), BF16),
        vmem((total_modes, samples * chan), BF16),
        vmem((owned, rows8, chan), F32),
        vmem((owned, rows8, chan), F32),
        vmem((owned, rows8, chan), F32),
        vmem(backwards + (rows_each, wide), BF16),
        pltpu.SemaphoreType.DMA((2 * samples + 5, load_steps)),
        pltpu.SemaphoreType.DMA((copies,)),
        pltpu.SemaphoreType.DMA((copies,)),
    ]

    def stage_buffers(radices, tail, first_type, later_type):
        return [
            vmem(shape + tail, later_type if turn else first_type)
            for turn, shape in enumerate(staged(radices, size))
        ]

    coef_tail, weight_tail = (owned, 2 * chan), (rows_each, wide)
    for first, later in ((F32, F32), (BF16, BF16), (F32, BF16)):
        for _ in range(samples):
            scratch += stage_buffers(reduce, coef_tail, first, later)
    for first, later in ((F32, F32), (BF16, BF16), (F32, BF16)):
        scratch += stage_buffers(gather, weight_tail, first, later)
    scratch += [vmem((shape[0], 1, hidden_units), F32) for shape in staged(gather, size)]
    outside = pl.BlockSpec(memory_space=pltpu.HBM)
    inside = pl.BlockSpec(memory_space=pltpu.VMEM)
    results = pl.pallas_call(
        functools.partial(layer_kernel, plan),
        out_shape=(
            jax.ShapeDtypeStruct((samples, here, chan), BF16),
            jax.ShapeDtypeStruct((owned, chan, chan), F32),
            jax.ShapeDtypeStruct((chan, hidden_units), F32),
            jax.ShapeDtypeStruct((1, hidden_units), F32),
            jax.ShapeDtypeStruct((chan, hidden_units), F32),
        ),
        in_specs=[outside] * 7,
        out_specs=(inside,) * 5,
        scratch_shapes=scratch,
        compiler_params=pltpu.CompilerParams(
            collective_id=0, has_side_effects=True, vmem_limit_bytes=45 * 1024 * 1024
        ),
        name="layer",
    )(*(pltpu.with_memory_space_constraint(x, pltpu.HBM) for x in (
        inputs, cotangent, basis, mode_weights, w_up, b_up.reshape(1, hidden_units), w_down)))
    grad_input, grad_modes, grad_up, grad_bias, grad_down = pl.pallas_call(
        place_kernel,
        out_shape=(
            jax.ShapeDtypeStruct((samples, here, chan), BF16),
            jax.ShapeDtypeStruct((owned, chan, chan), F32),
            jax.ShapeDtypeStruct((chan, hidden_units), F32),
            jax.ShapeDtypeStruct((1, hidden_units), F32),
            jax.ShapeDtypeStruct((hidden_units, chan), F32),
        ),
        in_specs=[inside] * 5,
        out_specs=(outside,) * 5,
        scratch_shapes=[vmem((hidden_units, chan), F32), pltpu.SemaphoreType.DMA((2 * 2 + 3,))],
        compiler_params=pltpu.CompilerParams(vmem_limit_bytes=8 * 1024 * 1024),
        name="place",
    )(*results)
    return grad_input, grad_modes, grad_up, grad_bias.reshape(hidden_units), grad_down


def solution(mesh):
    size = mesh.shape["vert"]
    groups = mesh.shape["samp"]

    def body(*arguments):
        grad_input, grad_modes, grad_up, grad_bias, grad_down = per_device(size, *arguments)
        if groups > 1:
            grad_modes, grad_up, grad_bias, grad_down = lax.psum(
                (grad_modes, grad_up, grad_bias, grad_down), "samp"
            )
        return grad_input, grad_modes, grad_up, grad_bias, grad_down

    in_specs = (
        P("samp", "vert", None),
        P("samp", "vert", None),
        P("vert", None),
        P("vert", None, None),
        P(),
        P(),
        P(),
    )
    out_specs = (P("samp", "vert", None), P("vert", None, None), P(), P(), P())
    return jax.shard_map(body, mesh=mesh, in_specs=in_specs, out_specs=out_specs, check_vma=False)
```
